256 devices in a mesh: wall: 2 (over z_lo), plane: 128 (over x, y, z_hi, core).
Axes of the slice: x: 4, y: 4, z: 8 (z_hi: 4, z_lo: 2; z = z_hi * 2 + z_lo), core: 2. Of those that a mesh axis runs over, the one named last changes fastest.
Arguments:
- jacobian: float32 [3, 16, 16, 32, 128, 128], P(None, None, None, 'wall', 'plane'), as said below
- residual: float32 [16, 32, 128, 128], P(None, 'wall', 'plane')
- previous_update: float32 [16, 32, 128, 128], P(None, 'wall', 'plane'), may hold values from -6 to 6
- offline_coupling: float32 [4, 16, 32, 128, 128], P(None, None, 'wall', 'plane'), may hold values from 0.003 to 0.03
- wake_partner: int32 [128, 128], P('plane'), may hold values from 0 to 127, each once within a row
- line_length: int32 [128, 128], P('plane'), may hold values from 16 to 32
- bottom_flag: int32 [128, 128], P('plane'), may hold values 0 or 1
Outputs:
- update: float32 [16, 32, 128, 128], P(None, 'wall', 'plane')
The draws below stay inside these ranges and needn't reach their ends.
Inputs may be any that keep to these rules, and one draw needn't show every extreme that they name: jacobian[2, :, :, k] is the transpose of jacobian[0, :, :, k + 1], every jacobian[1, :, :, k] is symmetric, and every row of a line's matrix is strictly diagonally dominant with a positive diagonal. `bottom_flag`: 1 where a column's first cell lies on the wake cut, 0 where it lies on the capsule wall. `wake_partner`: for a wake-cut column (i, j), the spanwise index of the column at station (i + 64) modulo 128, on the other branch of the cut, that lies beneath its first cell; each row is a permutation of 0 to 127.
All inputs are finite; a program needn't handle non-finite values. No bound on the sum of `bottom_flag` on one device may be relied on, other than what follows from the above.
Results may differ from the reference program's by a relative error of at most 0.0003.
Values sent between devices are 32-bit elements; how exact they have to be, the bound alone decides.
No kernel may reach another device: no remote copies, remote signals or barrier semaphores. Data moves between devices by JAX's collectives and lax.ppermute only.
A program may use at most 192 MiB of HBM per device.

```python
import math
import jax
import jax.numpy as jnp
from jax import lax

NV = 16
NJ = 128
NK = 32
NI = 128


def draw_jacobian(key, part):
    identity = jnp.eye(NV, dtype=jnp.float32)[:, :, None, None, None]
    samples = jax.random.uniform(jax.random.fold_in(key, 1), (NV, NV, NK + 1, NI, NJ), jnp.float32)
    coupling = -(0.6 * identity + 0.1 * samples)
    lower = coupling[:, :, :NK]
    upper = jnp.swapaxes(coupling[:, :, 1:], 0, 1)
    mixing_draw = jax.random.uniform(jax.random.fold_in(key, 2), (NV, NV, NK, NI, NJ), jnp.float32)
    mixing = -0.05 * (mixing_draw + jnp.swapaxes(mixing_draw, 0, 1)) * (1.0 - identity)
    margin = jnp.exp(jax.random.uniform(jax.random.fold_in(key, 3), (NV, NK, NI, NJ), jnp.float32, math.log(0.001), math.log(0.01)))
    total = jnp.sum(jnp.abs(lower), axis=1) + jnp.sum(jnp.abs(upper), axis=1) + jnp.sum(jnp.abs(mixing), axis=1) + margin
    middle = mixing + identity * total[:, None]
    return jnp.stack([lower, middle, upper])


def draw_residual(key, part):
    extent = (NV, NK, NI, NJ)
    return 0.05 * jax.random.normal(jax.random.fold_in(key, 11), extent, jnp.float32)


def plant(array, own_key, least, top_value):
    dims = array.shape
    place = [jax.random.randint(jax.random.fold_in(own_key, axis), (), 0, dims[axis]) for axis in range(len(dims))]
    array = array.at[tuple(place)].set(least)
    longest = dims.index(max(dims))
    place[longest] = (place[longest] + 1) % dims[longest]
    return array.at[tuple(place)].set(top_value)


def level_of(key, shape, split, smallest, largest):
    factor_of = 1.0
    for axis_at, blocks in split:
        draws = jax.random.uniform(jax.random.fold_in(jax.random.fold_in(key, 6), axis_at), (blocks,), jnp.float32, smallest / len(split), largest / len(split))
        factor_of = factor_of * jnp.repeat(jnp.exp(draws), shape[axis_at] // blocks).reshape((-1,) + (1,) * (len(shape) - 1 - axis_at))
    return factor_of


def bell_draw(key, dims, deviation, most, shards=(), kind=jnp.bfloat16):
    drawn = deviation * jax.random.normal(key, dims, jnp.float32)
    if shards:
        drawn = drawn * level_of(key, dims, shards, -0.22, 0.18)
    return jnp.clip(drawn, -most, most).astype(kind)


def setup_inputs(seed: int = 0) -> dict:
    splits = jax.random.split(jax.random.key(seed), 8)
    return {
        "jacobian": draw_jacobian(jax.random.fold_in(splits[7], 71), 0),
        "residual": draw_residual(jax.random.fold_in(splits[7], 71), 0),
        "previous_update": bell_draw(splits[2], (NV, NK, NI, NJ), 1.0, 6.0, ((1, 2), (2, 128)), jnp.float32),
        "offline_coupling": jnp.clip(jnp.exp(math.log(0.03) - 2.3025851 * jax.random.uniform(splits[3], (4, NV, NK, NI, NJ), jnp.float32) ** level_of(splits[3], (4, NV, NK, NI, NJ), ((2, 2), (3, 128)), -0.2, 0.2)), 0.003, 0.03),
        "wake_partner": jax.vmap(lambda own: jax.random.permutation(own, NJ))(jax.random.split(splits[4], NI)).reshape((NI, NJ)).astype(jnp.int32),
        "line_length": plant(jax.random.randint(splits[5], (NI, NJ), NK // 2, NK + 1), jax.random.fold_in(splits[5], 1), NK // 2, NK).astype(jnp.int32),
        "bottom_flag": plant((jax.random.randint(splits[6], (NI, NJ), 0, 2) < 1).astype(jnp.int32), jax.random.fold_in(splits[6], 1), 0, 1),
    }


precise = lax.Precision.HIGHEST


def product(left, right):
    return jnp.einsum("vwc,wuc->vuc", left, right, precision=precise)


def solve_block(matrix, given):
    extent = matrix.shape[0]
    augmented = jnp.concatenate([matrix, given], axis=1)
    for pivot in range(extent):
        pivot_row = augmented[pivot] / augmented[pivot, pivot][None, :]
        augmented = augmented - augmented[:, pivot][:, None, :] * pivot_row[None]
        augmented = augmented.at[pivot].set(pivot_row)
    return augmented[:, extent:]


def effective(lower, middle, upper, active_here, active_above, not_bottom):
    identity = jnp.eye(lower.shape[0], dtype=jnp.float32)[:, :, None, None]
    return (lower * (active_here * not_bottom)[None, None],
            middle * active_here[None, None] + identity * (1.0 - active_here)[None, None],
            upper * active_above[None, None])


def eliminate(lower, middle, upper, source, block_in, vector_in, levels):
    extent = lower.shape[0]
    blocks = jnp.zeros(lower.shape, jnp.float32)
    vectors = jnp.zeros(source.shape, jnp.float32)

    def advance(level, state):
        block_prev, vector_prev, blocks, vectors = state
        below = lax.dynamic_index_in_dim(lower, level, 2, keepdims=False)
        centre = lax.dynamic_index_in_dim(middle, level, 2, keepdims=False)
        above = lax.dynamic_index_in_dim(upper, level, 2, keepdims=False)
        given = lax.dynamic_index_in_dim(source, level, 2, keepdims=False)
        schur = centre - product(below, block_prev)
        reduced = given - product(below, vector_prev)
        joined = solve_block(schur, jnp.concatenate([above, reduced], axis=1))
        block_next = joined[:, :extent]
        vector_next = joined[:, extent:]
        blocks = lax.dynamic_update_index_in_dim(blocks, block_next, level, 2)
        vectors = lax.dynamic_update_index_in_dim(vectors, vector_next, level, 2)
        return block_next, vector_next, blocks, vectors

    return lax.fori_loop(0, levels, advance, (block_in, vector_in, blocks, vectors))


def substitute(blocks, vectors, value_above, levels, result):
    def retreat(count, state):
        value_next, result = state
        level = levels - 1 - count
        block = lax.dynamic_index_in_dim(blocks, level, 2, keepdims=False)
        vector = lax.dynamic_index_in_dim(vectors, level, 2, keepdims=False)
        value = vector - product(block, value_next)
        result = lax.dynamic_update_index_in_dim(result, value, level, 2)
        return value, result

    return lax.fori_loop(0, levels, retreat, (value_above, result))


def reference(jacobian, residual, previous_update, offline_coupling, wake_partner, line_length, bottom_flag):
    padded = jnp.pad(previous_update, ((0, 0), (0, 0), (1, 1), (0, 0)))
    offline = (offline_coupling[0] * padded[:, :, :-2] + offline_coupling[1] * padded[:, :, 2:]
               + offline_coupling[2] * jnp.roll(previous_update, 1, axis=3)
               + offline_coupling[3] * jnp.roll(previous_update, -1, axis=3))
    mirrored = jnp.roll(previous_update[:, 0], NI // 2, axis=1)
    partner = jnp.take_along_axis(mirrored, wake_partner.astype(jnp.int32)[None], axis=2)
    wake = jnp.einsum("vwij,wij->vij", jacobian[0, :, :, 0], partner, precision=precise)
    wake = wake * bottom_flag.astype(jnp.float32)[None]
    levels = jnp.arange(NK, dtype=jnp.int32)
    active = (levels[:, None, None] < line_length[None]).astype(jnp.float32)
    active_above = ((levels + 1)[:, None, None] < line_length[None]).astype(jnp.float32)
    not_bottom = (levels > 0).astype(jnp.float32)[:, None]
    source = residual + offline
    source = source.at[:, 0].add(-wake)
    source = source * active[None]

    def station(index):
        blocks = lax.dynamic_index_in_dim(jacobian, index, 4, keepdims=False)
        here = lax.dynamic_index_in_dim(active, index, 1, keepdims=False)
        above = lax.dynamic_index_in_dim(active_above, index, 1, keepdims=False)
        given = lax.dynamic_index_in_dim(source, index, 2, keepdims=False)[:, None]
        lower, middle, upper = effective(blocks[0], blocks[1], blocks[2], here, above, not_bottom)
        empty_block = jnp.zeros((NV, NV, NJ), jnp.float32)
        empty_vector = jnp.zeros((NV, 1, NJ), jnp.float32)
        parts = eliminate(lower, middle, upper, given, empty_block, empty_vector, NK)
        solved = substitute(parts[2], parts[3], empty_vector, NK, jnp.zeros(given.shape, jnp.float32))
        return solved[1][:, 0]

    stacked = lax.map(station, jnp.arange(NI, dtype=jnp.int32))
    return jnp.moveaxis(stacked, 0, 2)
```

```python
import jax
import jax.numpy as jnp
from jax import lax
from jax.experimental import pallas as pl
from jax.experimental.pallas import tpu as pltpu
from jax.sharding import PartitionSpec as P


N = 16
T = 16
LANES = 128
F32 = jnp.float32


def spread(row, lane):
    return jnp.broadcast_to(row[lane:lane + 1, :], (8, LANES))


def repeat(ref, row):
    return ref[pl.ds(row, 8, stride=0), :]


def pair(ref, base):
    return ref[pl.ds(base, 8), :], ref[pl.ds(base + 8, 8), :]


def total(terms):
    terms = list(terms)
    while len(terms) > 1:
        terms = [a + b for a, b in zip(terms[::2], terms[1::2])] + terms[len(terms) & ~1:]
    return terms[0]


def coupled(lo, hi, w_ref, v_ref):
    lo, hi = list(lo), list(hi)
    v = [pair(v_ref, p * N) for p in range(N)]
    for r in range(N):
        m = [repeat(w_ref, p * N + r) for p in range(N)]
        if r < 8:
            lo[r] = lo[r] - total(m[p] * v[p][0] for p in range(N))
        hi[r] = hi[r] - total(m[p] * v[p][1] for p in range(N))
    return lo, hi


def forward(lo, hi, wlo, whi, u_put, i_put, w_ref, v_ref):
    lo, hi, wlo, whi = list(lo), list(hi), list(wlo), list(whi)
    for q in range(N // 2):
        p0, p1 = 2 * q, 2 * q + 1
        own = lo if p0 < 8 else hi
        s = p0 % 8
        r0, r1 = own[p0], own[p1]
        h0, h1 = hi[p0], hi[p1]
        a, b, c = spread(r0, s), spread(r0, s + 1), spread(r1, s + 1)
        r = 1.0 / (a * c - b * b)
        i00, i01, i11 = c * r, -(b * r), a * r
        i_put(q, (i00, i01, i11))

        def norm(x):
            return i00 * x[p0] + i01 * x[p1], i01 * x[p0] + i11 * x[p1]

        uhi = norm(hi)
        ulo = norm(lo) if p0 < 8 else None
        vlo, vhi = norm(wlo), norm(whi)
        for k, p in enumerate((p0, p1)):
            u_put(p, ulo[k] if p0 < 8 else None, uhi[k])
            w_ref[pl.ds(p * N, 8), :] = wlo[p]
            w_ref[pl.ds(p * N + 8, 8), :] = whi[p]
            v_ref[pl.ds(p * N, 8), :] = vlo[k]
            v_ref[pl.ds(p * N + 8, 8), :] = vhi[k]
        for v in range(p1 + 1, N):
            if v < 8:
                m0, m1 = spread(r0, v), spread(r1, v)
                lo[v] = lo[v] - (m0 * ulo[0] + m1 * ulo[1])
            else:
                m0, m1 = spread(h0, v - 8), spread(h1, v - 8)
            hi[v] = hi[v] - (m0 * uhi[0] + m1 * uhi[1])
            wlo[v] = wlo[v] - (m0 * vlo[0] + m1 * vlo[1])
            whi[v] = whi[v] - (m0 * vhi[0] + m1 * vhi[1])


def backward(u_ref, u_base, v_ref, g_ref, g_base):
    g = [list(pair(v_ref, p * N)) for p in range(N)]
    for q in reversed(range(N // 2)):
        for p in (2 * q, 2 * q + 1):
            for v in range(2 * q + 2, N):
                m = repeat(u_ref, u_base + p * N + v)
                g[p][0] = g[p][0] - m * g[v][0]
                g[p][1] = g[p][1] - m * g[v][1]
    for p in range(N):
        g_ref[pl.ds(g_base + p * N, 8), :] = g[p][0]
        g_ref[pl.ds(g_base + p * N + 8, 8), :] = g[p][1]


def going_up():
    return lax.axis_index("wall") == 0


def factor_kernel(
    jac, length_ref, g_ref, u_ref, i_ref, s_ref, p_ref, m_buf, c_buf, w_a, v_a, w_b, v_b, m_sem, c_sem
):
    up = going_up()
    side = jnp.where(up, 2, 0)

    def copies(t):
        lev = jnp.where(up, t, T - 1 - t)
        return (
            pltpu.make_async_copy(jac.at[1, :, :, lev, 0, :], m_buf.at[t], m_sem.at[t]),
            pltpu.make_async_copy(jac.at[side, :, :, lev, 0, :], c_buf.at[t], c_sem.at[t]),
        )

    for t in range(T):
        for copy in copies(t):
            copy.start()
    length = jnp.broadcast_to(length_ref[...], (8, LANES))
    sub = lax.broadcasted_iota(jnp.int32, (8, LANES), 0)
    zero = jnp.zeros((8, LANES), F32)
    w_b[...] = jnp.zeros(w_b.shape, F32)
    v_b[...] = jnp.zeros(v_b.shape, F32)

    def level(t, w_p, v_p, w_t, v_t):
        for copy in copies(t):
            copy.wait()
        active = jnp.where(up, 0, 2 * T - 1 - t) < length
        linked = jnp.where(up, t + 1, 2 * T - 1 - t) < length
        lo, hi, wlo, whi = [], [], [], []
        for r in range(N):
            eye = jnp.where(sub == r % 8, 1.0, 0.0)
            if r < 8:
                lo.append(jnp.where(active, m_buf[t, r, 0:8, :], eye))
            hi.append(jnp.where(active, m_buf[t, r, 8:16, :], zero if r < 8 else eye))
            wlo.append(jnp.where(linked, c_buf[t, r, 0:8, :], 0.0))
            whi.append(jnp.where(linked, c_buf[t, r, 8:16, :], 0.0))
        lo, hi = coupled(lo, hi, w_p, v_p)
        for r in range(N):
            if r < 8:
                s_ref[pl.ds(r * N, 8), :] = lo[r]
            s_ref[pl.ds(r * N + 8, 8), :] = hi[r]

        def u_put(p, low, high):
            if low is not None:
                u_ref[pl.ds(t * 256 + p * N, 8), :] = low
            u_ref[pl.ds(t * 256 + p * N + 8, 8), :] = high

        def i_put(q, values):
            for k, value in enumerate(values):
                i_ref[pl.ds(t * 24 + q * 3 + k, 1), :] = value[0:1, :]

        forward(lo, hi, wlo, whi, u_put, i_put, w_t, v_t)
        backward(u_ref, t * 256, v_t, g_ref, t * 256)

    def body(h, carry):
        level(2 * h, w_b, v_b, w_a, v_a)
        level(2 * h + 1, w_a, v_a, w_b, v_b)
        return carry

    lax.fori_loop(0, T // 2, body, 0)
    lo, hi = coupled([zero] * 8, [zero] * N, w_b, v_b)
    for r in range(N):
        p_ref[pl.ds(r * N, 8), :] = lo[r] if r < 8 else zero
        p_ref[pl.ds(r * N + 8, 8), :] = hi[r]


def source_kernel(
    jac, residual, here, before, after, coupling, face, partner_ref, length_ref, flag_ref, g_ref,
    y_ref, q_ref, s_buf, k_buf, k_sem
):
    up = going_up()
    copy = pltpu.make_async_copy(jac.at[0, :, :, 0, 0, :], k_buf, k_sem)
    copy.start()
    length = jnp.broadcast_to(length_ref[...], (8, LANES))
    sub = lax.broadcasted_iota(jnp.int32, (8, LANES), 0)
    active = [jnp.where(up, 0, T) + 8 * h + sub < length for h in range(2)]
    for r in range(N):
        for h in range(2):
            at = pl.ds(r * T + 8 * h, 8)
            c = [coupling[pl.ds(m * N * T + r * T + 8 * h, 8), :] for m in range(4)]
            own = here[at, :]
            value = residual[at, :] + (
                (c[0] * before[at, :] + c[1] * after[at, :])
                + (c[2] * pltpu.roll(own, 1, 1) + c[3] * pltpu.roll(own, LANES - 1, 1))
            )
            s_buf[at, :] = jnp.where(active[h], value, 0.0)

    index = jnp.broadcast_to(partner_ref[...], (8, LANES))
    facing = [jnp.take_along_axis(face[pl.ds(8 * h, 8), :], index, axis=1) for h in range(2)]
    copy.wait()
    rows = k_buf.reshape(N * N, LANES)
    weight = jnp.broadcast_to(flag_ref[...].astype(F32), (8, LANES)) * jnp.where(up, 1.0, 0.0)

    def at_level(t):
        lev = jnp.where(up, t, T - 1 - t)
        return [s_buf[pl.ds(lev + 8 * h * T, 8, stride=T), :] for h in range(2)]

    m = [spread(facing[w // 8], w % 8) for w in range(N)]
    y = at_level(0)
    for h in range(2):
        wake = total(rows[pl.ds(h * 8 * N + w, 8, stride=N), :] * m[w] for w in range(N))
        y[h] = y[h] - weight * wake
    for t in range(T):
        for h in range(2):
            y_ref[pl.ds(8 * h * T + t, 8, stride=T), :] = y[h]
        m = [spread(y[p // 8], p % 8) for p in range(N)]
        sums = [total(g_ref[pl.ds(t * 256 + p * N + 8 * h, 8), :] * m[p] for p in range(N)) for h in range(2)]
        if t + 1 < T:
            y = [a - b for a, b in zip(at_level(t + 1), sums)]
        else:
            for h in range(2):
                q_ref[pl.ds(8 * h, 8), :] = sums[h]


def inner_kernel(u_ref, i_ref, y_ref, s_ref, p_ref, x_ref, inv_ref, w_buf, v_buf, u_buf):
    for h in range(2):
        def u(p, v):
            return u_ref[pl.ds(h * 8 * 256 + p * N + v, 8, stride=256), :]

        def i(q, k):
            return i_ref[pl.ds(h * 8 * 24 + q * 3 + k, 8, stride=24), :]

        y = [y_ref[pl.ds(p * T + 8 * h, 8), :] for p in range(N)]
        z = [None] * N
        for q in range(N // 2):
            p0, p1 = 2 * q, 2 * q + 1
            for v in range(p1 + 1, N):
                y[v] = y[v] - (u(p0, v) * y[p0] + u(p1, v) * y[p1])
            i00, i01, i11 = i(q, 0), i(q, 1), i(q, 2)
            z[p0] = i00 * y[p0] + i01 * y[p1]
            z[p1] = i01 * y[p0] + i11 * y[p1]
        for q in reversed(range(N // 2)):
            for p in (2 * q, 2 * q + 1):
                for v in range(2 * q + 2, N):
                    z[p] = z[p] - u(p, v) * z[v]
        for p in range(N):
            x_ref[pl.ds(p * T + 8 * h, 8), :] = z[p]

    sub = lax.broadcasted_iota(jnp.int32, (8, LANES), 0)
    zero = jnp.zeros((8, LANES), F32)
    lo = [s_ref[pl.ds(r * N, 8), :] + p_ref[pl.ds(r * N, 8), :] for r in range(8)]
    hi = [s_ref[pl.ds(r * N + 8, 8), :] + p_ref[pl.ds(r * N + 8, 8), :] for r in range(N)]
    eye = [jnp.where(sub == r, 1.0, 0.0) for r in range(8)]

    def u_put(p, low, high):
        if low is not None:
            u_buf[pl.ds(p * N, 8), :] = low
        u_buf[pl.ds(p * N + 8, 8), :] = high

    forward(lo, hi, eye + [zero] * 8, [zero] * 8 + eye, u_put, lambda q, v: None, w_buf, v_buf)
    backward(u_buf, 0, v_buf, inv_ref, 0)


def outer_kernel(g_ref, x0_ref, inv_ref, y_ref, q_ref, x_ref):
    up = going_up()
    last = T - 1
    rhs = [y_ref[pl.ds(8 * h * T + last, 8, stride=T), :] - q_ref[pl.ds(8 * h, 8), :] for h in range(2)]
    m = [spread(rhs[p // 8], p % 8) for p in range(N)]
    x = [total(inv_ref[pl.ds(p * N + 8 * h, 8), :] * m[p] for p in range(N)) for h in range(2)]
    for t in reversed(range(T)):
        if t < last:
            m = [spread(x[v // 8], v % 8) for v in range(N)]
            x = [
                x0_ref[pl.ds(8 * h * T + t, 8, stride=T), :]
                - total(g_ref[pl.ds(t * 256 + 8 * h * N + v, 8, stride=N), :] * m[v] for v in range(N))
                for h in range(2)
            ]
        lev = jnp.where(up, t, last - t)
        for h in range(2):
            x_ref[pl.ds(lev + 8 * h * T, 8, stride=T), :] = x[h]


def shape(rows):
    return jax.ShapeDtypeStruct((rows, LANES), F32)


ANY = pl.BlockSpec(memory_space=pl.ANY)
LOCAL = pl.BlockSpec(memory_space=pltpu.VMEM)


def call(kernel, name, outs, ins, scratch, args, flops):
    return pl.pallas_call(
        kernel,
        out_shape=tuple(shape(rows) for rows in outs),
        in_specs=ins,
        out_specs=[LOCAL] * len(outs),
        scratch_shapes=scratch,
        compiler_params=pltpu.CompilerParams(vmem_limit_bytes=24 * 2**20),
        cost_estimate=pl.CostEstimate(flops=flops, bytes_accessed=4 * 2**20, transcendentals=0),
        name=name,
    )(*args)


def per_device(
    jacobian, residual, previous_update, offline_coupling, wake_partner, line_length, bottom_flag
):
    planes = lax.axis_size("plane")
    block = pltpu.VMEM((N * N, LANES), F32)
    here = previous_update.reshape(N * T, LANES)
    forth = [(i, i + 1) for i in range(planes - 1)]
    before = lax.ppermute(here, "plane", forth)
    after = lax.ppermute(here, "plane", [(b, a) for a, b in forth])
    face = lax.ppermute(
        previous_update[:, 0, 0], "plane", [(i, (i + planes // 2) % planes) for i in range(planes)]
    )
    g, u, i, s, p = call(
        factor_kernel,
        "factor",
        (T * 256, T * 256, T * 24, 256, 256),
        [ANY, LOCAL],
        [pltpu.VMEM((T, N, N, LANES), F32)] * 2
        + [block] * 4
        + [pltpu.SemaphoreType.DMA((T,))] * 2,
        (jacobian, line_length),
        T * 128 * 2 * 12000,
    )
    swap = [(0, 1), (1, 0)]
    p = lax.ppermute(p, "wall", swap)
    y, q = call(
        source_kernel,
        "source",
        (256, 16),
        [ANY] + [LOCAL] * 10,
        [block, pltpu.VMEM((N, N, LANES), F32), pltpu.SemaphoreType.DMA],
        (
            jacobian,
            residual.reshape(N * T, LANES),
            here,
            before,
            after,
            offline_coupling.reshape(4 * N * T, LANES),
            face,
            wake_partner,
            line_length,
            bottom_flag,
            g,
        ),
        T * 128 * 2 * 800,
    )
    q = lax.ppermute(q, "wall", swap)
    x, inverse = call(
        inner_kernel, "inner", (256, 256), [LOCAL] * 5, [block] * 3, (u, i, y, s, p), T * 128 * 2 * 1000
    )
    (update,) = call(
        outer_kernel, "outer", (256,), [LOCAL] * 5, [], (g, x, inverse, y, q), T * 128 * 2 * 300
    )
    return update.reshape(N, T, 1, LANES)


def solution(mesh):
    return jax.shard_map(
        per_device,
        mesh=mesh,
        in_specs=(
            P(None, None, None, "wall", "plane", None),
            P(None, "wall", "plane", None),
            P(None, "wall", "plane", None),
            P(None, None, "wall", "plane", None),
            P("plane", None),
            P("plane", None),
            P("plane", None),
        ),
        out_specs=P(None, "wall", "plane", None),
        check_vma=False,
    )
```

```python
import jax
import jax.numpy as jnp
from jax import lax
from jax.experimental import pallas as pl
from jax.experimental.pallas import tpu as pltpu
from jax.sharding import PartitionSpec as P


N = 16
T = 16
LANES = 128
F32 = jnp.float32


def spread(row, lane):
    return jnp.broadcast_to(row[lane:lane + 1, :], (8, LANES))


def repeat(ref, row):
    return ref[pl.ds(row, 8, stride=0), :]


def pair(ref, base):
    return ref[pl.ds(base, 8), :], ref[pl.ds(base + 8, 8), :]


def total(terms):
    terms = list(terms)
    while len(terms) > 1:
        terms = [a + b for a, b in zip(terms[::2], terms[1::2])] + terms[len(terms) & ~1:]
    return terms[0]


def coupled(lo, hi, w_ref, v_ref, linked):
    lo, hi = list(lo), list(hi)
    v = [pair(v_ref, p * N) for p in range(N)]
    for r in range(N):
        m = [repeat(w_ref, p * N + r) for p in range(N)]
        if r < 8:
            lo[r] = lo[r] - jnp.where(linked, total(m[p] * v[p][0] for p in range(N)), 0.0)
        hi[r] = hi[r] - jnp.where(linked, total(m[p] * v[p][1] for p in range(N)), 0.0)
    return lo, hi


def forward(lo, hi, wlo, whi, u_put, i_put, w_ref, v_ref, b_ref):
    lo, hi, wlo, whi = list(lo), list(hi), list(wlo), list(whi)
    for q in range(N // 2):
        p0, p1, p2 = 2 * q, 2 * q + 1, 2 * q + 2
        own = lo if p0 < 8 else hi
        s = p0 % 8
        a, b, c = spread(own[p0], s), spread(own[p0], s + 1), spread(own[p1], s + 1)
        for p in (p0, p1):
            if p0 < 8:
                b_ref[pl.ds(p * N, 8), :] = lo[p]
            b_ref[pl.ds(p * N + 8, 8), :] = hi[p]
        r = 1.0 / (a * c - b * b)
        i00, i01, i11 = c * r, -(b * r), a * r
        i_put(q, (i00, i01, i11))

        def norm(x):
            return i00 * x[p0] + i01 * x[p1], i01 * x[p0] + i11 * x[p1]

        uhi = norm(hi)
        ulo = norm(lo) if p0 < 8 else None
        vlo, vhi = norm(wlo), norm(whi)
        for k, p in enumerate((p0, p1)):
            u_put(p, ulo[k] if p0 < 8 else None, uhi[k])
            w_ref[pl.ds(p * N, 8), :] = wlo[p]
            w_ref[pl.ds(p * N + 8, 8), :] = whi[p]
            v_ref[pl.ds(p * N, 8), :] = vlo[k]
            v_ref[pl.ds(p * N + 8, 8), :] = vhi[k]
        for v in range(p2, N):
            m0, m1 = repeat(b_ref, p0 * N + v), repeat(b_ref, p1 * N + v)
            if v < 8:
                lo[v] = lo[v] - (m0 * ulo[0] + m1 * ulo[1])
            hi[v] = hi[v] - (m0 * uhi[0] + m1 * uhi[1])
            wlo[v] = wlo[v] - (m0 * vlo[0] + m1 * vlo[1])
            whi[v] = whi[v] - (m0 * vhi[0] + m1 * vhi[1])


def backward(u_ref, u_base, v_ref, g_ref, g_base):
    g = [list(pair(v_ref, p * N)) for p in range(N)]
    for q in reversed(range(N // 2)):
        for p in (2 * q, 2 * q + 1):
            for v in range(2 * q + 2, N):
                m = repeat(u_ref, u_base + p * N + v)
                g[p][0] = g[p][0] - m * g[v][0]
                g[p][1] = g[p][1] - m * g[v][1]
    for p in range(N):
        g_ref[pl.ds(g_base + p * N, 8), :] = g[p][0]
        g_ref[pl.ds(g_base + p * N + 8, 8), :] = g[p][1]


def going_up():
    return lax.axis_index("wall") == 0


AHEAD = 4


def factor_kernel(
    jac, length_hbm,
    g_ref, u_ref, i_ref, s_ref, p_ref, k_ref,
    m_buf, c_buf, w_a, v_a, w_b, v_b, b_ref, l_buf, m_sem, c_sem, k_sem, l_sem
):
    up = going_up()
    side = jnp.where(up, 2, 0)

    def copies(t):
        lev = jnp.where(up, t, T - 1 - t)
        return (
            pltpu.make_async_copy(jac.at[1, :, :, lev, 0, :], m_buf.at[t], m_sem.at[t]),
            pltpu.make_async_copy(jac.at[side, :, :, lev, 0, :], c_buf.at[t], c_sem.at[t]),
        )

    def fetch(t):
        for copy in copies(t):
            copy.start()

    length_copy = pltpu.make_async_copy(length_hbm, l_buf, l_sem)
    length_copy.start()
    for t in range(AHEAD):
        fetch(t)
    wake_copy = pltpu.make_async_copy(jac.at[0, :, :, 0, 0, :], k_ref, k_sem)
    zero = jnp.zeros((8, LANES), F32)
    w_b[...] = jnp.zeros(w_b.shape, F32)
    v_b[...] = jnp.zeros(v_b.shape, F32)
    length_copy.wait()

    def linked(t):
        return jnp.where(up, t + 1, 2 * T - 1 - t) < jnp.broadcast_to(l_buf[...], (8, LANES))

    def level(t, w_p, v_p, w_t, v_t):
        for copy in copies(t):
            copy.wait()
        lo, hi, wlo, whi = [], [], [], []
        for r in range(N):
            lo.append(m_buf[t, r, 0:8, :])
            hi.append(m_buf[t, r, 8:16, :])
            wlo.append(c_buf[t, r, 0:8, :])
            whi.append(c_buf[t, r, 8:16, :])
        lo, hi = coupled(lo[:8], hi, w_p, v_p, linked(t - 1))
        for r in range(N):
            if r < 8:
                s_ref[pl.ds(r * 8, 8), :] = lo[r]
            s_ref[pl.ds(64 + r * 8, 8), :] = hi[r]

        def u_put(p, low, high):
            if low is not None:
                u_ref[pl.ds(t * 256 + p * N, 8), :] = low
            u_ref[pl.ds(t * 256 + p * N + 8, 8), :] = high

        def i_put(q, values):
            for k, value in enumerate(values):
                i_ref[pl.ds(t * 24 + q * 3 + k, 1), :] = value[0:1, :]

        forward(lo, hi, wlo, whi, u_put, i_put, w_t, v_t, b_ref)
        backward(u_ref, t * 256, v_t, g_ref, t * 256)

    def body(h, carry):
        @pl.when(h < (T - AHEAD) // 2)
        def _():
            fetch(2 * h + AHEAD)
            fetch(2 * h + AHEAD + 1)

        @pl.when(h == (T - AHEAD) // 2)
        def _():
            wake_copy.start()

        level(2 * h, w_b, v_b, w_a, v_a)
        level(2 * h + 1, w_a, v_a, w_b, v_b)
        return carry

    lax.fori_loop(0, T // 2, body, 0)
    lo, hi = coupled([zero] * 8, [zero] * N, w_b, v_b, linked(T - 1))
    for r, row in enumerate(lo + hi):
        p_ref[pl.ds(r * 8, 8), :] = row
    wake_copy.wait()


def source_kernel(
    k_buf, residual, here, face, near, far, coupling, partner_ref, length_ref, flag_ref, g_ref,
    y_ref, q_ref, s_buf
):
    up = going_up()
    length = jnp.broadcast_to(length_ref[...], (8, LANES))
    sub = lax.broadcasted_iota(jnp.int32, (8, LANES), 0)
    odd = lax.axis_index("plane") % 2
    active = [jnp.where(up, 0, T) + 8 * h + sub < length for h in range(2)]
    for r in range(N):
        for h in range(2):
            at = pl.ds(r * T + 8 * h, 8)
            c = [
                coupling[pl.ds(m * (N * T) + (r * T + 8 * h), 8), :]
                for m in (1 - odd, odd, 2, 3)
            ]
            own = here[at, :]
            value = residual[at, :] + (
                (c[0] * near[at, :] + c[1] * far[at, :])
                + (c[2] * pltpu.roll(own, 1, 1) + c[3] * pltpu.roll(own, LANES - 1, 1))
            )
            s_buf[at, :] = jnp.where(active[h], value, 0.0)

    index = jnp.broadcast_to(partner_ref[...], (8, LANES))
    facing = [jnp.take_along_axis(face[pl.ds(8 * h * 16, 8, stride=16), :], index, axis=1) for h in range(2)]
    weight = jnp.broadcast_to(flag_ref[...].astype(F32), (8, LANES)) * jnp.where(up, 1.0, 0.0)

    def at_level(t):
        lev = jnp.where(up, t, T - 1 - t)
        return [s_buf[pl.ds(lev + 8 * h * T, 8, stride=T), :] for h in range(2)]

    m = [spread(facing[w // 8], w % 8) for w in range(N)]
    y = at_level(0)
    for h in range(2):
        wake = total(k_buf[pl.ds(h * 8 * N + w, 8, stride=N), :] * m[w] for w in range(N))
        y[h] = y[h] - weight * wake
    for t in range(T):
        for h in range(2):
            y_ref[pl.ds(8 * h * T + t, 8, stride=T), :] = y[h]
        m = [spread(y[p // 8], p % 8) for p in range(N)]
        linked = jnp.where(up, t + 1, 2 * T - 1 - t) < length
        sums = [
            jnp.where(linked, total(g_ref[pl.ds(t * 256 + p * N + 8 * h, 8), :] * m[p] for p in range(N)), 0.0)
            for h in range(2)
        ]
        if t + 1 < T:
            y = [a - b for a, b in zip(at_level(t + 1), sums)]
        else:
            for h in range(2):
                q_ref[pl.ds(8 * h, 8), :] = sums[h]


def inner_kernel(u_ref, i_ref, g_ref, y_ref, x_ref, turned_ref):
    def turn(t, carry):
        for v in range(N):
            for h in range(2):
                column = g_ref[pl.ds(t * 256 + 8 * h * N + v, 8, stride=N), :]
                turned_ref[pl.ds(t * 256 + v * N + 8 * h, 8), :] = column
        return carry

    lax.fori_loop(0, T, turn, 0)
    for h in range(2):
        def u(p, v):
            return u_ref[pl.ds(h * 8 * 256 + p * N + v, 8, stride=256), :]

        def i(q, k):
            return i_ref[pl.ds(h * 8 * 24 + q * 3 + k, 8, stride=24), :]

        y = [y_ref[pl.ds(p * T + 8 * h, 8), :] for p in range(N)]
        z = [None] * N
        for q in range(N // 2):
            p0, p1 = 2 * q, 2 * q + 1
            for v in range(p1 + 1, N):
                y[v] = y[v] - (u(p0, v) * y[p0] + u(p1, v) * y[p1])
            i00, i01, i11 = i(q, 0), i(q, 1), i(q, 2)
            z[p0] = i00 * y[p0] + i01 * y[p1]
            z[p1] = i01 * y[p0] + i11 * y[p1]
        for q in reversed(range(N // 2)):
            for p in (2 * q, 2 * q + 1):
                for v in range(2 * q + 2, N):
                    z[p] = z[p] - u(p, v) * z[v]
        for p in range(N):
            x_ref[pl.ds(p * T + 8 * h, 8), :] = z[p]


def outer_kernel(
    s_ref, p_ref, turned_ref, x0_ref, y_ref, length_ref, q_ref, x_ref, inv_ref, w_buf, v_buf, u_buf, b_buf
):
    sub = lax.broadcasted_iota(jnp.int32, (8, LANES), 0)
    zero = jnp.zeros((8, LANES), F32)
    rows = [s_ref[pl.ds(r * 8, 8), :] + p_ref[pl.ds(r * 8, 8), :] for r in range(24)]
    lo, hi = rows[:8], rows[8:]
    eye = [jnp.where(sub == r, 1.0, 0.0) for r in range(8)]

    def u_put(p, low, high):
        if low is not None:
            u_buf[pl.ds(p * N, 8), :] = low
        u_buf[pl.ds(p * N + 8, 8), :] = high

    forward(lo, hi, eye + [zero] * 8, [zero] * 8 + eye, u_put, lambda q, v: None, w_buf, v_buf, b_buf)
    backward(u_buf, 0, v_buf, inv_ref, 0)
    up = going_up()
    length = jnp.broadcast_to(length_ref[...], (8, LANES))
    last = T - 1
    rhs = [y_ref[pl.ds(8 * h * T + last, 8, stride=T), :] - q_ref[pl.ds(8 * h, 8), :] for h in range(2)]
    m = [spread(rhs[p // 8], p % 8) for p in range(N)]
    x = [total(inv_ref[pl.ds(p * N + 8 * h, 8), :] * m[p] for p in range(N)) for h in range(2)]
    for t in reversed(range(T)):
        if t < last:
            m = [spread(x[v // 8], v % 8) for v in range(N)]
            x = [
                x0_ref[pl.ds(8 * h * T + t, 8, stride=T), :]
                - total(turned_ref[pl.ds(t * 256 + v * N + 8 * h, 8), :] * m[v] for v in range(N))
                for h in range(2)
            ]
        active = jnp.where(up, 0, 2 * T - 1 - t) < length
        x = [jnp.where(active, value, 0.0) for value in x]
        lev = jnp.where(up, t, last - t)
        for h in range(2):
            x_ref[pl.ds(lev + 8 * h * T, 8, stride=T), :] = x[h]


ANY = pl.BlockSpec(memory_space=pltpu.HBM)
LOCAL = pl.BlockSpec(memory_space=pltpu.VMEM)


def call(kernel, name, outs, ins, scratch, args, flops, limit=24):
    return pl.pallas_call(
        kernel,
        out_shape=tuple(
            jax.ShapeDtypeStruct(rows + (LANES,) if isinstance(rows, tuple) else (rows, LANES), F32)
            for rows in outs
        ),
        in_specs=ins,
        out_specs=[LOCAL] * len(outs),
        scratch_shapes=scratch,
        compiler_params=pltpu.CompilerParams(vmem_limit_bytes=limit * 2**20),
        cost_estimate=pl.CostEstimate(flops=flops, bytes_accessed=4 * 2**20, transcendentals=0),
        name=name,
    )(*args)


def factor(jacobian, line_length):
    block = pltpu.VMEM((N * N, LANES), F32)
    return call(
        factor_kernel,
        "factor",
        (T * 256, T * 256, T * 24, 192, 192, (N, N)),
        [ANY, ANY],
        [pltpu.VMEM((T, N, N, LANES), F32)] * 2
        + [block] * 5
        + [pltpu.VMEM((1, LANES), jnp.int32)]
        + [pltpu.SemaphoreType.DMA((T,))] * 2
        + [pltpu.SemaphoreType.DMA] * 2,
        (jacobian, line_length),
        10**10,
        48,
    )


def per_device(
    jacobian, residual, previous_update, offline_coupling, wake_partner, line_length, bottom_flag
):
    planes = lax.axis_size("plane")
    block = pltpu.VMEM((N * N, LANES), F32)
    here = previous_update.reshape(N * T, LANES)
    face = lax.ppermute(
        previous_update[:, :16].reshape(N * 16, LANES),
        ("wall", "plane"),
        [(i, (i + planes // 2) % planes) for i in range(planes)],
    )
    near = lax.ppermute(here, "plane", [(i, i ^ 1) for i in range(planes)])
    across = [(i, i + 1) for i in range(1, planes - 1, 2)]
    far = lax.ppermute(here, "plane", across + [(b, a) for a, b in across])
    g, u, i, s, p, k = factor(
        jacobian, pltpu.with_memory_space_constraint(line_length, pltpu.HBM)
    )
    swap = [(0, 1), (1, 0)]
    p = lax.ppermute(p, "wall", swap)
    y, q = call(
        source_kernel,
        "source",
        (256, 16),
        [LOCAL] * 11,
        [block],
        (
            k.reshape(N * N, LANES),
            residual.reshape(N * T, LANES),
            here,
            face,
            near,
            far,
            offline_coupling.reshape(4 * N * T, LANES),
            wake_partner,
            line_length,
            bottom_flag,
            g,
        ),
        10**9,
    )
    q = lax.ppermute(q, "wall", swap)
    x, turned = call(
        inner_kernel, "inner", (256, T * 256), [LOCAL] * 4, [], (u, i, g, y), 2 * 10**9
    )
    (update,) = call(
        outer_kernel,
        "outer",
        (256,),
        [LOCAL] * 7,
        [block] * 5,
        (s, p, turned, x, y, line_length, q),
        10**9,
    )
    return update.reshape(N, T, 1, LANES)


def solution(mesh):
    return jax.shard_map(
        per_device,
        mesh=mesh,
        in_specs=(
            P(None, None, None, "wall", "plane", None),
            P(None, "wall", "plane", None),
            P(None, "wall", "plane", None),
            P(None, None, "wall", "plane", None),
            P("plane", None),
            P("plane", None),
            P("plane", None),
        ),
        out_specs=P(None, "wall", "plane", None),
        check_vma=False,
    )
```

```python
import jax
import jax.numpy as jnp
from jax import lax
from jax.experimental import pallas as pl
from jax.experimental.pallas import tpu as pltpu
from jax.sharding import PartitionSpec as P


N = 16
T = 16
LANES = 128
F32 = jnp.float32


def spread(row, lane):
    return jnp.broadcast_to(row[lane:lane + 1, :], (8, LANES))


def repeat(ref, row):
    return ref[pl.ds(row, 8, stride=0), :]


def pair(ref, base):
    return ref[pl.ds(base, 8), :], ref[pl.ds(base + 8, 8), :]


def total(terms):
    terms = list(terms)
    while len(terms) > 1:
        terms = [a + b for a, b in zip(terms[::2], terms[1::2])] + terms[len(terms) & ~1:]
    return terms[0]


def coupled(lo, hi, w_ref, v_ref, linked):
    lo, hi = list(lo), list(hi)
    v = [pair(v_ref, p * N) for p in range(N)]
    for r in range(N):
        m = [repeat(w_ref, p * N + r) for p in range(N)]
        if r < 8:
            lo[r] = lo[r] - jnp.where(linked, total(m[p] * v[p][0] for p in range(N)), 0.0)
        hi[r] = hi[r] - jnp.where(linked, total(m[p] * v[p][1] for p in range(N)), 0.0)
    return lo, hi


def forward(lo, hi, wlo, whi, u_put, i_put, w_ref, v_ref, b_ref):
    lo, hi, wlo, whi = list(lo), list(hi), list(wlo), list(whi)
    for q in range(N // 2):
        p0, p1, p2 = 2 * q, 2 * q + 1, 2 * q + 2
        own = lo if p0 < 8 else hi
        s = p0 % 8
        a, b, c = spread(own[p0], s), spread(own[p0], s + 1), spread(own[p1], s + 1)
        for p in (p0, p1):
            if p0 < 8:
                b_ref[pl.ds(p * N, 8), :] = lo[p]
            b_ref[pl.ds(p * N + 8, 8), :] = hi[p]
        r = 1.0 / (a * c - b * b)
        i00, i01, i11 = c * r, -(b * r), a * r
        i_put(q, (i00, i01, i11))

        def norm(x):
            return i00 * x[p0] + i01 * x[p1], i01 * x[p0] + i11 * x[p1]

        uhi = norm(hi)
        ulo = norm(lo) if p0 < 8 else None
        vlo, vhi = norm(wlo), norm(whi)
        for k, p in enumerate((p0, p1)):
            u_put(p, ulo[k] if p0 < 8 else None, uhi[k])
            w_ref[pl.ds(p * N, 8), :] = wlo[p]
            w_ref[pl.ds(p * N + 8, 8), :] = whi[p]
            v_ref[pl.ds(p * N, 8), :] = vlo[k]
            v_ref[pl.ds(p * N + 8, 8), :] = vhi[k]
        for v in range(p2, N):
            m0, m1 = repeat(b_ref, p0 * N + v), repeat(b_ref, p1 * N + v)
            if v < 8:
                lo[v] = lo[v] - (m0 * ulo[0] + m1 * ulo[1])
            hi[v] = hi[v] - (m0 * uhi[0] + m1 * uhi[1])
            wlo[v] = wlo[v] - (m0 * vlo[0] + m1 * vlo[1])
            whi[v] = whi[v] - (m0 * vhi[0] + m1 * vhi[1])


def backward(u_ref, u_base, v_ref, g_ref, g_base):
    g = [list(pair(v_ref, p * N)) for p in range(N)]
    for q in reversed(range(N // 2)):
        for p in (2 * q, 2 * q + 1):
            for v in range(2 * q + 2, N):
                m = repeat(u_ref, u_base + p * N + v)
                g[p][0] = g[p][0] - m * g[v][0]
                g[p][1] = g[p][1] - m * g[v][1]
    for p in range(N):
        g_ref[pl.ds(g_base + p * N, 8), :] = g[p][0]
        g_ref[pl.ds(g_base + p * N + 8, 8), :] = g[p][1]


def going_up():
    return lax.axis_index("wall") == 0


AHEAD = 4
EARLY = 6


def is_early():
    return lax.axis_index("plane") // 2 % 4 == 0


def linked(t, length_ref):
    return jnp.where(going_up(), t + 1, 2 * T - 1 - t) < jnp.broadcast_to(length_ref[...], (8, LANES))


def eliminate(first, last, jac, l_buf, g_ref, u_ref, i_ref, s_ref, odd, buffers, at_step):
    m_buf, c_buf, w_a, v_a, b_ref, m_sem, c_sem = buffers
    w_b, v_b = odd
    up = going_up()
    side = jnp.where(up, 2, 0)

    def copies(t):
        lev = jnp.where(up, t, T - 1 - t)
        return (
            pltpu.make_async_copy(jac.at[1, :, :, lev, 0, :], m_buf.at[t], m_sem.at[t]),
            pltpu.make_async_copy(jac.at[side, :, :, lev, 0, :], c_buf.at[t], c_sem.at[t]),
        )

    def fetch(t):
        for copy in copies(t):
            copy.start()

    def level(t, w_p, v_p, w_t, v_t):
        for copy in copies(t):
            copy.wait()
        lo, hi, wlo, whi = [], [], [], []
        for r in range(N):
            lo.append(m_buf[t, r, 0:8, :])
            hi.append(m_buf[t, r, 8:16, :])
            wlo.append(c_buf[t, r, 0:8, :])
            whi.append(c_buf[t, r, 8:16, :])
        lo, hi = coupled(lo[:8], hi, w_p, v_p, linked(t - 1, l_buf))
        if s_ref is not None:
            for r in range(N):
                if r < 8:
                    s_ref[pl.ds(r * 8, 8), :] = lo[r]
                s_ref[pl.ds(64 + r * 8, 8), :] = hi[r]

        def u_put(p, low, high):
            if low is not None:
                u_ref[pl.ds(t * 256 + p * N, 8), :] = low
            u_ref[pl.ds(t * 256 + p * N + 8, 8), :] = high

        def i_put(q, values):
            for k, value in enumerate(values):
                i_ref[pl.ds(t * 24 + q * 3 + k, 1), :] = value[0:1, :]

        forward(lo, hi, wlo, whi, u_put, i_put, w_t, v_t, b_ref)
        backward(u_ref, t * 256, v_t, g_ref, t * 256)

    def body(h, carry):
        @pl.when(h < last - AHEAD // 2)
        def _():
            fetch(2 * h + AHEAD)
            fetch(2 * h + AHEAD + 1)

        at_step(h)
        level(2 * h, w_b, v_b, w_a, v_a)
        level(2 * h + 1, w_a, v_a, w_b, v_b)
        return carry

    return fetch, lambda: lax.fori_loop(first, last, body, 0)


def early_kernel(
    jac, length_hbm, g_ref, u_ref, i_ref, w_ref, v_ref, m_buf, c_buf, w_a, v_a, b_ref, l_buf, m_sem, c_sem, l_sem
):
    @pl.when(is_early())
    def _():
        length_copy = pltpu.make_async_copy(length_hbm, l_buf, l_sem)
        length_copy.start()
        buffers = m_buf, c_buf, w_a, v_a, b_ref, m_sem, c_sem
        fetch, run = eliminate(
            0, EARLY, jac, l_buf, g_ref, u_ref, i_ref, None, (w_ref, v_ref), buffers, lambda h: None
        )
        for t in range(AHEAD):
            fetch(t)
        w_ref[...] = jnp.zeros(w_ref.shape, F32)
        v_ref[...] = jnp.zeros(v_ref.shape, F32)
        length_copy.wait()
        run()


def factor_kernel(
    jac, length_hbm, g_in, u_in, i_in, w_in, v_in,
    g_ref, u_ref, i_ref, s_ref, p_ref, k_ref,
    m_buf, c_buf, w_a, v_a, b_ref, w_b, v_b, l_buf, m_sem, c_sem, k_sem, l_sem, e_sem
):
    early = is_early()
    zero = jnp.zeros((8, LANES), F32)
    length_copy = pltpu.make_async_copy(length_hbm, l_buf, l_sem)
    wake_copy = pltpu.make_async_copy(jac.at[0, :, :, 0, 0, :], k_ref, k_sem)
    state_copies = [
        pltpu.make_async_copy(w_in, w_b, e_sem.at[0]),
        pltpu.make_async_copy(v_in, v_b, e_sem.at[1]),
    ]
    done_copies = [
        pltpu.make_async_copy(g_in, g_ref.at[pl.ds(0, EARLY * 512)], e_sem.at[2]),
        pltpu.make_async_copy(u_in, u_ref.at[pl.ds(0, EARLY * 512)], e_sem.at[3]),
        pltpu.make_async_copy(i_in, i_ref.at[pl.ds(0, EARLY * 48)], e_sem.at[4]),
    ]

    def at_step(h):
        @pl.when(h == (T - AHEAD) // 2)
        def _():
            wake_copy.start()

    buffers = m_buf, c_buf, w_a, v_a, b_ref, m_sem, c_sem
    first = jnp.where(early, EARLY, 0)
    fetch, run = eliminate(
        first, T // 2, jac, l_buf, g_ref, u_ref, i_ref, s_ref, (w_b, v_b), buffers, at_step
    )
    length_copy.start()

    @pl.when(early)
    def _():
        for copy in state_copies:
            copy.start()

    for t in range(AHEAD):
        fetch(2 * first + t)

    @pl.when(early)
    def _():
        for copy in done_copies:
            copy.start()
        for copy in state_copies:
            copy.wait()

    @pl.when(jnp.logical_not(early))
    def _():
        w_b[...] = jnp.zeros(w_b.shape, F32)
        v_b[...] = jnp.zeros(v_b.shape, F32)

    length_copy.wait()
    run()
    lo, hi = coupled([zero] * 8, [zero] * N, w_b, v_b, linked(T - 1, l_buf))
    for r, row in enumerate(lo + hi):
        p_ref[pl.ds(r * 8, 8), :] = row

    @pl.when(early)
    def _():
        for copy in done_copies:
            copy.wait()

    wake_copy.wait()


def source_kernel(
    k_buf, residual, here, far, near, face, coupling, partner_ref, length_ref, flag_ref, g_ref,
    y_ref, q_ref, s_buf
):
    up = going_up()
    length = jnp.broadcast_to(length_ref[...], (8, LANES))
    sub = lax.broadcasted_iota(jnp.int32, (8, LANES), 0)
    odd = lax.axis_index("plane") % 2
    active = [jnp.where(up, 0, T) + 8 * h + sub < length for h in range(2)]
    for r in range(N):
        for h in range(2):
            at = pl.ds(r * T + 8 * h, 8)
            c = [
                coupling[pl.ds(m * (N * T) + (r * T + 8 * h), 8), :]
                for m in (1 - odd, odd, 2, 3)
            ]
            own = here[at, :]
            value = residual[at, :] + (
                (c[0] * near[at, :] + c[1] * far[at, :])
                + (c[2] * pltpu.roll(own, 1, 1) + c[3] * pltpu.roll(own, LANES - 1, 1))
            )
            s_buf[at, :] = jnp.where(active[h], value, 0.0)

    index = jnp.broadcast_to(partner_ref[...], (8, LANES))
    facing = [jnp.take_along_axis(face[pl.ds(8 * h * 16, 8, stride=16), :], index, axis=1) for h in range(2)]
    weight = jnp.broadcast_to(flag_ref[...].astype(F32), (8, LANES)) * jnp.where(up, 1.0, 0.0)

    def at_level(t):
        lev = jnp.where(up, t, T - 1 - t)
        return [s_buf[pl.ds(lev + 8 * h * T, 8, stride=T), :] for h in range(2)]

    m = [spread(facing[w // 8], w % 8) for w in range(N)]
    y = at_level(0)
    for h in range(2):
        wake = total(k_buf[pl.ds(h * 8 * N + w, 8, stride=N), :] * m[w] for w in range(N))
        y[h] = y[h] - weight * wake
    for t in range(T):
        for h in range(2):
            y_ref[pl.ds(8 * h * T + t, 8, stride=T), :] = y[h]
        m = [spread(y[p // 8], p % 8) for p in range(N)]
        linked = jnp.where(up, t + 1, 2 * T - 1 - t) < length
        sums = [
            jnp.where(linked, total(g_ref[pl.ds(t * 256 + p * N + 8 * h, 8), :] * m[p] for p in range(N)), 0.0)
            for h in range(2)
        ]
        if t + 1 < T:
            y = [a - b for a, b in zip(at_level(t + 1), sums)]
        else:
            for h in range(2):
                q_ref[pl.ds(8 * h, 8), :] = sums[h]


def inner_kernel(u_ref, i_ref, g_ref, y_ref, x_ref, turned_ref):
    def turn(t, carry):
        for v in range(N):
            for h in range(2):
                column = g_ref[pl.ds(t * 256 + 8 * h * N + v, 8, stride=N), :]
                turned_ref[pl.ds(t * 256 + v * N + 8 * h, 8), :] = column
        return carry

    lax.fori_loop(0, T, turn, 0)
    for h in range(2):
        def u(p, v):
            return u_ref[pl.ds(h * 8 * 256 + p * N + v, 8, stride=256), :]

        def i(q, k):
            return i_ref[pl.ds(h * 8 * 24 + q * 3 + k, 8, stride=24), :]

        y = [y_ref[pl.ds(p * T + 8 * h, 8), :] for p in range(N)]
        z = [None] * N
        for q in range(N // 2):
            p0, p1 = 2 * q, 2 * q + 1
            for v in range(p1 + 1, N):
                y[v] = y[v] - (u(p0, v) * y[p0] + u(p1, v) * y[p1])
            i00, i01, i11 = i(q, 0), i(q, 1), i(q, 2)
            z[p0] = i00 * y[p0] + i01 * y[p1]
            z[p1] = i01 * y[p0] + i11 * y[p1]
        for q in reversed(range(N // 2)):
            for p in (2 * q, 2 * q + 1):
                for v in range(2 * q + 2, N):
                    z[p] = z[p] - u(p, v) * z[v]
        for p in range(N):
            x_ref[pl.ds(p * T + 8 * h, 8), :] = z[p]


def outer_kernel(
    s_ref, p_ref, turned_ref, x0_ref, y_ref, length_ref, q_ref, x_ref, inv_ref, w_buf, v_buf, u_buf, b_buf
):
    sub = lax.broadcasted_iota(jnp.int32, (8, LANES), 0)
    zero = jnp.zeros((8, LANES), F32)
    rows = [s_ref[pl.ds(r * 8, 8), :] + p_ref[pl.ds(r * 8, 8), :] for r in range(24)]
    lo, hi = rows[:8], rows[8:]
    eye = [jnp.where(sub == r, 1.0, 0.0) for r in range(8)]

    def u_put(p, low, high):
        if low is not None:
            u_buf[pl.ds(p * N, 8), :] = low
        u_buf[pl.ds(p * N + 8, 8), :] = high

    forward(lo, hi, eye + [zero] * 8, [zero] * 8 + eye, u_put, lambda q, v: None, w_buf, v_buf, b_buf)
    backward(u_buf, 0, v_buf, inv_ref, 0)
    up = going_up()
    length = jnp.broadcast_to(length_ref[...], (8, LANES))
    last = T - 1
    rhs = [y_ref[pl.ds(8 * h * T + last, 8, stride=T), :] - q_ref[pl.ds(8 * h, 8), :] for h in range(2)]
    m = [spread(rhs[p // 8], p % 8) for p in range(N)]
    x = [total(inv_ref[pl.ds(p * N + 8 * h, 8), :] * m[p] for p in range(N)) for h in range(2)]
    for t in reversed(range(T)):
        if t < last:
            m = [spread(x[v // 8], v % 8) for v in range(N)]
            x = [
                x0_ref[pl.ds(8 * h * T + t, 8, stride=T), :]
                - total(turned_ref[pl.ds(t * 256 + v * N + 8 * h, 8), :] * m[v] for v in range(N))
                for h in range(2)
            ]
        active = jnp.where(up, 0, 2 * T - 1 - t) < length
        x = [jnp.where(active, value, 0.0) for value in x]
        lev = jnp.where(up, t, last - t)
        for h in range(2):
            x_ref[pl.ds(lev + 8 * h * T, 8, stride=T), :] = x[h]


ANY = pl.BlockSpec(memory_space=pltpu.HBM)
LOCAL = pl.BlockSpec(memory_space=pltpu.VMEM)


def call(kernel, name, outs, ins, scratch, args, flops, limit=24):
    return pl.pallas_call(
        kernel,
        out_shape=tuple(
            jax.ShapeDtypeStruct(rows + (LANES,) if isinstance(rows, tuple) else (rows, LANES), F32)
            for rows in outs
        ),
        in_specs=ins,
        out_specs=[LOCAL] * len(outs),
        scratch_shapes=scratch,
        compiler_params=pltpu.CompilerParams(vmem_limit_bytes=limit * 2**20),
        cost_estimate=pl.CostEstimate(flops=flops, bytes_accessed=4 * 2**20, transcendentals=0),
        name=name,
    )(*args)


def factor_early(jacobian, length):
    block = pltpu.VMEM((N * N, LANES), F32)
    return call(
        early_kernel,
        "early",
        (EARLY * 512, EARLY * 512, EARLY * 48, 256, 256),
        [ANY, ANY],
        [pltpu.VMEM((2 * EARLY, N, N, LANES), F32)] * 2
        + [block] * 3
        + [pltpu.VMEM((1, LANES), jnp.int32)]
        + [pltpu.SemaphoreType.DMA((2 * EARLY,))] * 2
        + [pltpu.SemaphoreType.DMA],
        (jacobian, length),
        10**10,
        46,
    )


def factor(jacobian, length, state):
    block = pltpu.VMEM((N * N, LANES), F32)
    return call(
        factor_kernel,
        "factor",
        (T * 256, T * 256, T * 24, 192, 192, (N, N)),
        [ANY] * 7,
        [pltpu.VMEM((T, N, N, LANES), F32)] * 2
        + [block] * 5
        + [pltpu.VMEM((1, LANES), jnp.int32)]
        + [pltpu.SemaphoreType.DMA((T,))] * 2
        + [pltpu.SemaphoreType.DMA] * 2
        + [pltpu.SemaphoreType.DMA((5,))],
        (jacobian, length, *state),
        10**10,
        46,
    )


def per_device(
    jacobian, residual, previous_update, offline_coupling, wake_partner, line_length, bottom_flag
):
    planes = lax.axis_size("plane")
    block = pltpu.VMEM((N * N, LANES), F32)
    length = pltpu.with_memory_space_constraint(line_length, pltpu.HBM)
    state = factor_early(jacobian, length)
    ready, *state = lax.optimization_barrier((previous_update, *state))
    here = ready.reshape(N * T, LANES)
    face = lax.ppermute(
        here,
        ("wall", "plane"),
        [(i, (i + planes // 2) % planes) for i in range(planes)],
    )
    near = lax.ppermute(here, "plane", [(i, i ^ 1) for i in range(planes)])
    across = [(i, i + 1) for i in range(1, planes - 1, 2)]
    far = lax.ppermute(here, "plane", across + [(b, a) for a, b in across])
    g, u, i, s, p, k = factor(jacobian, length, state)
    swap = [(0, 1), (1, 0)]
    p = lax.ppermute(p, "wall", swap)
    y, q = call(
        source_kernel,
        "source",
        (256, 16),
        [LOCAL] * 11,
        [block],
        (
            k.reshape(N * N, LANES),
            residual.reshape(N * T, LANES),
            here,
            far,
            near,
            face,
            offline_coupling.reshape(4 * N * T, LANES),
            wake_partner,
            line_length,
            bottom_flag,
            g,
        ),
        10**9,
    )
    q = lax.ppermute(q, "wall", swap)
    x, turned = call(
        inner_kernel, "inner", (256, T * 256), [LOCAL] * 4, [], (u, i, g, y), 2 * 10**9
    )
    (update,) = call(
        outer_kernel,
        "outer",
        (256,),
        [LOCAL] * 7,
        [block] * 5,
        (s, p, turned, x, y, line_length, q),
        10**9,
    )
    return update.reshape(N, T, 1, LANES)


def solution(mesh):
    return jax.shard_map(
        per_device,
        mesh=mesh,
        in_specs=(
            P(None, None, None, "wall", "plane", None),
            P(None, "wall", "plane", None),
            P(None, "wall", "plane", None),
            P(None, None, "wall", "plane", None),
            P("plane", None),
            P("plane", None),
            P("plane", None),
        ),
        out_specs=P(None, "wall", "plane", None),
        check_vma=False,
    )
```

```python
import jax
import jax.numpy as jnp
from jax import lax
from jax.experimental import pallas as pl
from jax.experimental.pallas import tpu as pltpu
from jax.sharding import PartitionSpec as P


N = 16
T = 16
LANES = 128
F32 = jnp.float32


def spread(row, lane):
    return jnp.broadcast_to(row[lane:lane + 1, :], (8, LANES))


def repeat(ref, row):
    return ref[pl.ds(row, 8, stride=0), :]


def pair(ref, base):
    return ref[pl.ds(base, 8), :], ref[pl.ds(base + 8, 8), :]


def total(terms):
    terms = list(terms)
    while len(terms) > 1:
        terms = [a + b for a, b in zip(terms[::2], terms[1::2])] + terms[len(terms) & ~1:]
    return terms[0]


def coupled(lo, hi, w_ref, v_ref, linked):
    lo, hi = list(lo), list(hi)
    v = [pair(v_ref, p * N) for p in range(N)]
    for r in range(N):
        m = [repeat(w_ref, p * N + r) for p in range(N)]
        if r < 8:
            lo[r] = lo[r] - jnp.where(linked, total(m[p] * v[p][0] for p in range(N)), 0.0)
        hi[r] = hi[r] - jnp.where(linked, total(m[p] * v[p][1] for p in range(N)), 0.0)
    return lo, hi


def forward(lo, hi, wlo, whi, u_put, i_put, w_ref, v_ref, b_ref):
    lo, hi, wlo, whi = list(lo), list(hi), list(wlo), list(whi)
    for q in range(N // 2):
        p0, p1, p2 = 2 * q, 2 * q + 1, 2 * q + 2
        own = lo if p0 < 8 else hi
        s = p0 % 8
        a, b, c = spread(own[p0], s), spread(own[p0], s + 1), spread(own[p1], s + 1)
        for p in (p0, p1):
            if p0 < 8:
                b_ref[pl.ds(p * N, 8), :] = lo[p]
            b_ref[pl.ds(p * N + 8, 8), :] = hi[p]
        r = 1.0 / (a * c - b * b)
        i00, i01, i11 = c * r, -(b * r), a * r
        i_put(q, (i00, i01, i11))

        def norm(x):
            return i00 * x[p0] + i01 * x[p1], i01 * x[p0] + i11 * x[p1]

        uhi = norm(hi)
        ulo = norm(lo) if p0 < 8 else None
        vlo, vhi = norm(wlo), norm(whi)
        for k, p in enumerate((p0, p1)):
            u_put(p, ulo[k] if p0 < 8 else None, uhi[k])
            w_ref[pl.ds(p * N, 8), :] = wlo[p]
            w_ref[pl.ds(p * N + 8, 8), :] = whi[p]
            v_ref[pl.ds(p * N, 8), :] = vlo[k]
            v_ref[pl.ds(p * N + 8, 8), :] = vhi[k]
        for v in range(p2, N):
            m0, m1 = repeat(b_ref, p0 * N + v), repeat(b_ref, p1 * N + v)
            if v < 8:
                lo[v] = lo[v] - (m0 * ulo[0] + m1 * ulo[1])
            hi[v] = hi[v] - (m0 * uhi[0] + m1 * uhi[1])
            wlo[v] = wlo[v] - (m0 * vlo[0] + m1 * vlo[1])
            whi[v] = whi[v] - (m0 * vhi[0] + m1 * vhi[1])


def backward(u_ref, u_base, v_ref, g_ref, g_base):
    g = [list(pair(v_ref, p * N)) for p in range(N)]
    for q in reversed(range(N // 2)):
        for p in (2 * q, 2 * q + 1):
            for v in range(2 * q + 2, N):
                m = repeat(u_ref, u_base + p * N + v)
                g[p][0] = g[p][0] - m * g[v][0]
                g[p][1] = g[p][1] - m * g[v][1]
    for p in range(N):
        g_ref[pl.ds(g_base + p * N, 8), :] = g[p][0]
        g_ref[pl.ds(g_base + p * N + 8, 8), :] = g[p][1]


def going_up():
    return lax.axis_index("wall") == 0


AHEAD = 4
EARLY = 6


def is_early():
    return lax.axis_index("plane") // 2 % 4 == 0


def linked(t, length_ref):
    return jnp.where(going_up(), t + 1, 2 * T - 1 - t) < jnp.broadcast_to(length_ref[...], (8, LANES))


def eliminate(first, last, jac, l_buf, g_ref, u_ref, i_ref, s_ref, odd, buffers, at_step):
    m_buf, c_buf, w_a, v_a, b_ref, m_sem, c_sem = buffers
    w_b, v_b = odd
    up = going_up()
    side = jnp.where(up, 2, 0)

    def copies(t):
        lev = jnp.where(up, t, T - 1 - t)
        return (
            pltpu.make_async_copy(jac.at[1, :, :, lev, 0, :], m_buf.at[t], m_sem.at[t]),
            pltpu.make_async_copy(jac.at[side, :, :, lev, 0, :], c_buf.at[t], c_sem.at[t]),
        )

    def fetch(t):
        for copy in copies(t):
            copy.start()

    def level(t, w_p, v_p, w_t, v_t):
        for copy in copies(t):
            copy.wait()
        lo, hi, wlo, whi = [], [], [], []
        for r in range(N):
            lo.append(m_buf[t, r, 0:8, :])
            hi.append(m_buf[t, r, 8:16, :])
            wlo.append(c_buf[t, r, 0:8, :])
            whi.append(c_buf[t, r, 8:16, :])
        lo, hi = coupled(lo[:8], hi, w_p, v_p, linked(t - 1, l_buf))
        if s_ref is not None:
            for r in range(N):
                if r < 8:
                    s_ref[pl.ds(r * 8, 8), :] = lo[r]
                s_ref[pl.ds(64 + r * 8, 8), :] = hi[r]

        def u_put(p, low, high):
            if low is not None:
                u_ref[pl.ds(t * 256 + p * N, 8), :] = low
            u_ref[pl.ds(t * 256 + p * N + 8, 8), :] = high

        def i_put(q, values):
            for k, value in enumerate(values):
                i_ref[pl.ds(t * 24 + q * 3 + k, 1), :] = value[0:1, :]

        forward(lo, hi, wlo, whi, u_put, i_put, w_t, v_t, b_ref)
        backward(u_ref, t * 256, v_t, g_ref, t * 256)

    def body(h, carry):
        @pl.when(h < last - AHEAD // 2)
        def _():
            fetch(2 * h + AHEAD)
            fetch(2 * h + AHEAD + 1)

        at_step(h)
        level(2 * h, w_b, v_b, w_a, v_a)
        level(2 * h + 1, w_a, v_a, w_b, v_b)
        return carry

    return fetch, lambda: lax.fori_loop(first, last, body, 0)


def early_kernel(
    jac, length_hbm, g_ref, u_ref, i_ref, w_ref, v_ref, m_buf, c_buf, w_a, v_a, b_ref, l_buf, m_sem, c_sem, l_sem
):
    @pl.when(is_early())
    def _():
        length_copy = pltpu.make_async_copy(length_hbm, l_buf, l_sem)
        length_copy.start()
        buffers = m_buf, c_buf, w_a, v_a, b_ref, m_sem, c_sem
        fetch, run = eliminate(
            0, EARLY, jac, l_buf, g_ref, u_ref, i_ref, None, (w_ref, v_ref), buffers, lambda h: None
        )
        for t in range(AHEAD):
            fetch(t)
        w_ref[...] = jnp.zeros(w_ref.shape, F32)
        v_ref[...] = jnp.zeros(v_ref.shape, F32)
        length_copy.wait()
        run()


def factor_kernel(
    jac, length_hbm, g_in, u_in, i_in, w_in, v_in,
    g_ref, u_ref, i_ref, s_ref, p_ref, k_ref,
    m_buf, c_buf, w_a, v_a, b_ref, w_b, v_b, l_buf, m_sem, c_sem, k_sem, l_sem, e_sem
):
    early = is_early()
    zero = jnp.zeros((8, LANES), F32)
    length_copy = pltpu.make_async_copy(length_hbm, l_buf, l_sem)
    wake_copy = pltpu.make_async_copy(jac.at[0, :, :, 0, 0, :], k_ref, k_sem)
    state_copies = [
        pltpu.make_async_copy(w_in, w_b, e_sem.at[0]),
        pltpu.make_async_copy(v_in, v_b, e_sem.at[1]),
    ]
    done_copies = [
        pltpu.make_async_copy(g_in, g_ref.at[pl.ds(0, EARLY * 512)], e_sem.at[2]),
        pltpu.make_async_copy(u_in, u_ref.at[pl.ds(0, EARLY * 512)], e_sem.at[3]),
        pltpu.make_async_copy(i_in, i_ref.at[pl.ds(0, EARLY * 48)], e_sem.at[4]),
    ]

    def at_step(h):
        @pl.when(h == (T - AHEAD) // 2)
        def _():
            wake_copy.start()

    buffers = m_buf, c_buf, w_a, v_a, b_ref, m_sem, c_sem
    first = jnp.where(early, EARLY, 0)
    fetch, run = eliminate(
        first, T // 2, jac, l_buf, g_ref, u_ref, i_ref, s_ref, (w_b, v_b), buffers, at_step
    )
    length_copy.start()

    @pl.when(early)
    def _():
        for copy in state_copies:
            copy.start()

    for t in range(AHEAD):
        fetch(2 * first + t)

    @pl.when(early)
    def _():
        for copy in done_copies:
            copy.start()
        for copy in state_copies:
            copy.wait()

    @pl.when(jnp.logical_not(early))
    def _():
        w_b[...] = jnp.zeros(w_b.shape, F32)
        v_b[...] = jnp.zeros(v_b.shape, F32)

    length_copy.wait()
    run()
    lo, hi = coupled([zero] * 8, [zero] * N, w_b, v_b, linked(T - 1, l_buf))
    sub = lax.broadcasted_iota(jnp.int32, (8, LANES), 0)
    corner = zero
    for r in range(8):
        p_ref[pl.ds(r * 8, 8), :] = jnp.where(sub >= r, lo[r], hi[8 + r])
        p_ref[pl.ds(64 + r * 8, 8), :] = hi[r]
        corner = jnp.where(sub == r, hi[8 + r], corner)
    p_ref[pl.ds(128, 8), :] = corner

    @pl.when(early)
    def _():
        for copy in done_copies:
            copy.wait()

    wake_copy.wait()


def source_kernel(
    k_buf, residual, here, far, near, face, coupling, partner_ref, length_ref, flag_ref, g_ref,
    y_ref, q_ref, s_buf
):
    up = going_up()
    length = jnp.broadcast_to(length_ref[...], (8, LANES))
    sub = lax.broadcasted_iota(jnp.int32, (8, LANES), 0)
    odd = lax.axis_index("plane") % 2
    active = [jnp.where(up, 0, T) + 8 * h + sub < length for h in range(2)]
    for r in range(N):
        for h in range(2):
            at = pl.ds(r * T + 8 * h, 8)
            c = [
                coupling[pl.ds(m * (N * T) + (r * T + 8 * h), 8), :]
                for m in (1 - odd, odd, 2, 3)
            ]
            own = here[at, :]
            value = residual[at, :] + (
                (c[0] * near[at, :] + c[1] * far[at, :])
                + (c[2] * pltpu.roll(own, 1, 1) + c[3] * pltpu.roll(own, LANES - 1, 1))
            )
            s_buf[at, :] = jnp.where(active[h], value, 0.0)

    index = jnp.broadcast_to(partner_ref[...], (8, LANES))
    facing = [jnp.take_along_axis(face[pl.ds(8 * h * 16, 8, stride=16), :], index, axis=1) for h in range(2)]
    weight = jnp.broadcast_to(flag_ref[...].astype(F32), (8, LANES)) * jnp.where(up, 1.0, 0.0)

    def at_level(t):
        lev = jnp.where(up, t, T - 1 - t)
        return [s_buf[pl.ds(lev + 8 * h * T, 8, stride=T), :] for h in range(2)]

    m = [spread(facing[w // 8], w % 8) for w in range(N)]
    y = at_level(0)
    for h in range(2):
        wake = total(k_buf[pl.ds(h * 8 * N + w, 8, stride=N), :] * m[w] for w in range(N))
        y[h] = y[h] - weight * wake
    for t in range(T):
        for h in range(2):
            y_ref[pl.ds(8 * h * T + t, 8, stride=T), :] = y[h]
        m = [spread(y[p // 8], p % 8) for p in range(N)]
        linked = jnp.where(up, t + 1, 2 * T - 1 - t) < length
        sums = [
            jnp.where(linked, total(g_ref[pl.ds(t * 256 + p * N + 8 * h, 8), :] * m[p] for p in range(N)), 0.0)
            for h in range(2)
        ]
        if t + 1 < T:
            y = [a - b for a, b in zip(at_level(t + 1), sums)]
        else:
            for h in range(2):
                q_ref[pl.ds(8 * h, 8), :] = sums[h]


def inner_kernel(u_ref, i_ref, g_ref, y_ref, x_ref, turned_ref):
    def turn(t, carry):
        for v in range(N):
            for h in range(2):
                column = g_ref[pl.ds(t * 256 + 8 * h * N + v, 8, stride=N), :]
                turned_ref[pl.ds(t * 256 + v * N + 8 * h, 8), :] = column
        return carry

    lax.fori_loop(0, T, turn, 0)
    for h in range(2):
        def u(p, v):
            return u_ref[pl.ds(h * 8 * 256 + p * N + v, 8, stride=256), :]

        def i(q, k):
            return i_ref[pl.ds(h * 8 * 24 + q * 3 + k, 8, stride=24), :]

        y = [y_ref[pl.ds(p * T + 8 * h, 8), :] for p in range(N)]
        z = [None] * N
        for q in range(N // 2):
            p0, p1 = 2 * q, 2 * q + 1
            for v in range(p1 + 1, N):
                y[v] = y[v] - (u(p0, v) * y[p0] + u(p1, v) * y[p1])
            i00, i01, i11 = i(q, 0), i(q, 1), i(q, 2)
            z[p0] = i00 * y[p0] + i01 * y[p1]
            z[p1] = i01 * y[p0] + i11 * y[p1]
        for q in reversed(range(N // 2)):
            for p in (2 * q, 2 * q + 1):
                for v in range(2 * q + 2, N):
                    z[p] = z[p] - u(p, v) * z[v]
        for p in range(N):
            x_ref[pl.ds(p * T + 8 * h, 8), :] = z[p]


def outer_kernel(
    s_ref, p_ref, turned_ref, x0_ref, y_ref, length_ref, q_ref, x_ref, inv_ref, w_buf, v_buf, u_buf, b_buf
):
    sub = lax.broadcasted_iota(jnp.int32, (8, LANES), 0)
    zero = jnp.zeros((8, LANES), F32)
    corner = p_ref[pl.ds(128, 8), :]
    rows = [p_ref[pl.ds(r * 8, 8), :] for r in range(16)]
    turned = [p_ref[pl.ds(r, 8, stride=8), :] for r in range(8)]
    first = [jnp.where(sub >= r, rows[r], turned[r]) for r in range(8)]
    second = [
        jnp.where(sub < r, rows[r], jnp.where(sub == r, corner, turned[r])) for r in range(8)
    ]
    rows = [s_ref[pl.ds(r * 8, 8), :] + row for r, row in enumerate(first + rows[8:] + second)]
    lo, hi = rows[:8], rows[8:]
    eye = [jnp.where(sub == r, 1.0, 0.0) for r in range(8)]

    def u_put(p, low, high):
        if low is not None:
            u_buf[pl.ds(p * N, 8), :] = low
        u_buf[pl.ds(p * N + 8, 8), :] = high

    forward(lo, hi, eye + [zero] * 8, [zero] * 8 + eye, u_put, lambda q, v: None, w_buf, v_buf, b_buf)
    backward(u_buf, 0, v_buf, inv_ref, 0)
    up = going_up()
    length = jnp.broadcast_to(length_ref[...], (8, LANES))
    last = T - 1
    rhs = [y_ref[pl.ds(8 * h * T + last, 8, stride=T), :] - q_ref[pl.ds(8 * h, 8), :] for h in range(2)]
    m = [spread(rhs[p // 8], p % 8) for p in range(N)]
    x = [total(inv_ref[pl.ds(p * N + 8 * h, 8), :] * m[p] for p in range(N)) for h in range(2)]
    for t in reversed(range(T)):
        if t < last:
            m = [spread(x[v // 8], v % 8) for v in range(N)]
            x = [
                x0_ref[pl.ds(8 * h * T + t, 8, stride=T), :]
                - total(turned_ref[pl.ds(t * 256 + v * N + 8 * h, 8), :] * m[v] for v in range(N))
                for h in range(2)
            ]
        active = jnp.where(up, 0, 2 * T - 1 - t) < length
        x = [jnp.where(active, value, 0.0) for value in x]
        lev = jnp.where(up, t, last - t)
        for h in range(2):
            x_ref[pl.ds(lev + 8 * h * T, 8, stride=T), :] = x[h]


ANY = pl.BlockSpec(memory_space=pltpu.HBM)
LOCAL = pl.BlockSpec(memory_space=pltpu.VMEM)


def call(kernel, name, outs, ins, scratch, args, flops, limit=24):
    return pl.pallas_call(
        kernel,
        out_shape=tuple(
            jax.ShapeDtypeStruct(rows + (LANES,) if isinstance(rows, tuple) else (rows, LANES), F32)
            for rows in outs
        ),
        in_specs=ins,
        out_specs=[LOCAL] * len(outs),
        scratch_shapes=scratch,
        compiler_params=pltpu.CompilerParams(vmem_limit_bytes=limit * 2**20),
        cost_estimate=pl.CostEstimate(flops=flops, bytes_accessed=4 * 2**20, transcendentals=0),
        name=name,
    )(*args)


def factor_early(jacobian, length):
    block = pltpu.VMEM((N * N, LANES), F32)
    return call(
        early_kernel,
        "early",
        (EARLY * 512, EARLY * 512, EARLY * 48, 256, 256),
        [ANY, ANY],
        [pltpu.VMEM((2 * EARLY, N, N, LANES), F32)] * 2
        + [block] * 3
        + [pltpu.VMEM((1, LANES), jnp.int32)]
        + [pltpu.SemaphoreType.DMA((2 * EARLY,))] * 2
        + [pltpu.SemaphoreType.DMA],
        (jacobian, length),
        10**10,
        46,
    )


def factor(jacobian, length, state):
    block = pltpu.VMEM((N * N, LANES), F32)
    return call(
        factor_kernel,
        "factor",
        (T * 256, T * 256, T * 24, 192, 136, (N, N)),
        [ANY] * 7,
        [pltpu.VMEM((T, N, N, LANES), F32)] * 2
        + [block] * 5
        + [pltpu.VMEM((1, LANES), jnp.int32)]
        + [pltpu.SemaphoreType.DMA((T,))] * 2
        + [pltpu.SemaphoreType.DMA] * 2
        + [pltpu.SemaphoreType.DMA((5,))],
        (jacobian, length, *state),
        10**10,
        46,
    )


def per_device(
    jacobian, residual, previous_update, offline_coupling, wake_partner, line_length, bottom_flag
):
    planes = lax.axis_size("plane")
    block = pltpu.VMEM((N * N, LANES), F32)
    length = pltpu.with_memory_space_constraint(line_length, pltpu.HBM)
    state = factor_early(jacobian, length)
    ready, *state = lax.optimization_barrier((previous_update, *state))
    here = ready.reshape(N * T, LANES)
    face = lax.ppermute(
        here,
        ("wall", "plane"),
        [(i, (i + planes // 2) % planes) for i in range(planes)],
    )
    near = lax.ppermute(here, "plane", [(i, i ^ 1) for i in range(planes)])
    across = [(i, i + 1) for i in range(1, planes - 1, 2)]
    far = lax.ppermute(here, "plane", across + [(b, a) for a, b in across])
    g, u, i, s, p, k = factor(jacobian, length, state)
    swap = [(0, 1), (1, 0)]
    p = lax.ppermute(p, "wall", swap)
    y, q = call(
        source_kernel,
        "source",
        (256, 16),
        [LOCAL] * 11,
        [block],
        (
            k.reshape(N * N, LANES),
            residual.reshape(N * T, LANES),
            here,
            far,
            near,
            face,
            offline_coupling.reshape(4 * N * T, LANES),
            wake_partner,
            line_length,
            bottom_flag,
            g,
        ),
        10**9,
    )
    q = lax.ppermute(q, "wall", swap)
    x, turned = call(
        inner_kernel, "inner", (256, T * 256), [LOCAL] * 4, [], (u, i, g, y), 2 * 10**9
    )
    (update,) = call(
        outer_kernel,
        "outer",
        (256,),
        [LOCAL] * 7,
        [block] * 5,
        (s, p, turned, x, y, line_length, q),
        10**9,
    )
    return update.reshape(N, T, 1, LANES)


def solution(mesh):
    return jax.shard_map(
        per_device,
        mesh=mesh,
        in_specs=(
            P(None, None, None, "wall", "plane", None),
            P(None, "wall", "plane", None),
            P(None, "wall", "plane", None),
            P(None, None, "wall", "plane", None),
            P("plane", None),
            P("plane", None),
            P("plane", None),
        ),
        out_specs=P(None, "wall", "plane", None),
        check_vma=False,
    )
```
